32 devices in a mesh: dp: 8 (over y, x, core), tensor: 4 (over z).
Axes of the slice: x: 2, y: 2, z: 4, core: 2. Of those that a mesh axis runs over, the one named last changes fastest.
Arguments:
- tokens: bfloat16 [8192, 2560], P(('dp', 'tensor')), may hold values from -6 to 6
- lengths: int32 [8], P('dp'), may hold values from 256 to 1024, as said below
- first_gain: float32 [2560], P('dp'), may hold values from 0.5 to 1.5
- query_weight: float32 [2560, 2560], P('dp', 'tensor'), may hold values from -0.25 to 0.25
- key_weight: float32 [2560, 640], P('dp', 'tensor'), may hold values from -0.125 to 0.125
- value_weight: float32 [2560, 640], P('dp', 'tensor'), may hold values from -0.125 to 0.125
- out_weight: float32 [2560, 2560], P('tensor', 'dp'), may hold values from -0.5 to 0.5
- second_gain: float32 [2560], P('dp'), may hold values from 0.5 to 1.5
- gate_weight: float32 [2560, 6912], P('dp', 'tensor'), may hold values from -0.125 to 0.125
- up_weight: float32 [2560, 6912], P('dp', 'tensor'), may hold values from -0.125 to 0.125
- down_weight: float32 [6912, 2560], P('tensor', 'dp'), may hold values from -0.078125 to 0.078125
- cotangent: bfloat16 [8192, 2560], P(('dp', 'tensor')), may hold values from -6 to 6
Outputs:
- block_out: bfloat16 [8192, 2560], P(('dp', 'tensor'))
- tokens_grad: float32 [8192, 2560], P(('dp', 'tensor'))
- first_grad: float32 [2560], P('dp')
- query_grad: float32 [2560, 2560], P('dp', 'tensor')
- key_grad: float32 [2560, 640], P('dp', 'tensor')
- value_grad: float32 [2560, 640], P('dp', 'tensor')
- out_grad: float32 [2560, 2560], P('tensor', 'dp')
- second_grad: float32 [2560], P('dp')
- gate_grad: float32 [2560, 6912], P('dp', 'tensor')
- up_grad: float32 [2560, 6912], P('dp', 'tensor')
- down_grad: float32 [6912, 2560], P('tensor', 'dp')
The draws below stay inside these ranges and needn't reach their ends.
Inputs may be any that keep to these rules, and one draw needn't show every extreme that they name: `lengths`: in every draw one sequence is full and one holds 256 valid positions.
All inputs are finite; a program needn't handle non-finite values.
Results may differ from the reference program's by a relative error of at most 0.02.
Values may be sent and summed in bfloat16 or wider, within the bound.
No kernel may reach another device: no remote copies, remote signals or barrier semaphores. Data moves between devices by JAX's collectives and lax.ppermute only.
A program may use at most 256 MiB of HBM per device.

```python
import math
import jax
import jax.numpy as jnp
from jax import lax

D = 2560
HEADS = 32
KV = 8
HD = 80
FF = 6912
LEN = 1024
NSEQ = 8
TOKENS = 8192


def draw_lengths(key, part):
    stream = jax.random.fold_in(key, 11)
    first_key, second_key, third_key = jax.random.split(stream, 3)
    drawn = jax.random.randint(first_key, (NSEQ,), LEN // 4, LEN + 1)
    full_at = jax.random.randint(second_key, (), 0, NSEQ)
    short_at = (full_at + 1 + jax.random.randint(third_key, (), 0, NSEQ - 1)) % NSEQ
    places = jnp.arange(NSEQ)
    drawn = jnp.where(places == full_at, LEN, drawn)
    return jnp.where(places == short_at, LEN // 4, drawn).astype(jnp.int32)


def block_levels(rng, dims, cuts, smallest, high):
    loudness = 1.0
    for dim, parts in cuts:
        draws = jax.random.uniform(jax.random.fold_in(jax.random.fold_in(rng, 6), dim), (parts,), jnp.float32, smallest / len(cuts), high / len(cuts))
        loudness = loudness * jnp.repeat(jnp.exp(draws), dims[dim] // parts).reshape((-1,) + (1,) * (len(dims) - 1 - dim))
    return loudness


def gaussian(key, dims, spread, bound, pieces=(), kind=jnp.bfloat16):
    values = jax.random.normal(key, dims, jnp.float32) * spread
    if len(pieces) > 0:
        values = block_levels(key, dims, pieces, -0.22, 0.18) * values
    return jnp.clip(values, min=-bound, max=bound).astype(kind)


def setup_inputs(seed: int = 0) -> dict:
    seeds = jax.random.split(jax.random.key(seed), 13)
    tokens = gaussian(seeds[0], (TOKENS, D), 1.0, 6.0, ((0, 32),))
    lengths = draw_lengths(jax.random.fold_in(seeds[12], 71), 0)
    first_gain = jnp.clip(1.0 + 0.1 * jax.random.normal(seeds[2], (D,), jnp.float32), 0.5, 1.5)
    query_weight = gaussian(seeds[3], (D, HEADS * HD), (D // 4) ** -0.5, 0.25, ((0, 8), (1, 4)), jnp.float32)
    key_weight = gaussian(seeds[4], (D, KV * HD), D ** -0.5, 0.125, ((0, 8), (1, 4)), jnp.float32)
    value_weight = gaussian(seeds[5], (D, KV * HD), D ** -0.5, 0.125, ((0, 8), (1, 4)), jnp.float32)
    out_weight = gaussian(seeds[6], (HEADS * HD, D), (HEADS * HD // 16) ** -0.5, 0.5, ((0, 4), (1, 8)), jnp.float32)
    second_gain = jnp.clip(1.0 + 0.1 * jax.random.normal(seeds[7], (D,), jnp.float32), 0.5, 1.5)
    gate_weight = gaussian(seeds[8], (D, FF), D ** -0.5, 0.125, ((0, 8), (1, 4)), jnp.float32)
    up_weight = gaussian(seeds[9], (D, FF), D ** -0.5, 0.125, ((0, 8), (1, 4)), jnp.float32)
    down_weight = gaussian(seeds[10], (FF, D), FF ** -0.5, 0.078125, ((0, 4), (1, 8)), jnp.float32)
    cotangent = gaussian(seeds[11], (TOKENS, D), 1.0, 6.0, ((0, 32),))
    return {"tokens": tokens, "lengths": lengths, "first_gain": first_gain, "query_weight": query_weight, "key_weight": key_weight, "value_weight": value_weight, "out_weight": out_weight, "second_gain": second_gain, "gate_weight": gate_weight, "up_weight": up_weight, "down_weight": down_weight, "cotangent": cotangent}


@jax.custom_vjp
def low(v):
    return lax.optimization_barrier(v.astype(jnp.bfloat16)).astype(jnp.float32)

@jax.custom_vjp
def low_back(v):
    return v

def low_keep(v):
    return (low(v), None)

def low_pass(kept, grad):
    return (grad,)

def back_keep(v):
    return (v, None)

def back_low(kept, grad):
    return (low(grad),)
low.defvjp(low_keep, low_pass)
low_back.defvjp(back_keep, back_low)
epsilon = 1e-05
rope_base = 10000.0
highest = lax.Precision.HIGHEST

def product(left, right):
    return jnp.dot(left, right, precision=highest, preferred_element_type=jnp.float32)

def rope_tables():
    half_dim = HD // 2
    freqs = rope_base ** (-(2.0 * jnp.arange(half_dim, dtype=jnp.float32)) / HD)
    angles = jnp.arange(LEN, dtype=jnp.float32)[:, None] * freqs[None, :]
    cosine = jnp.concatenate([jnp.cos(angles), jnp.cos(angles)], -1)
    sine = jnp.concatenate([jnp.sin(angles), jnp.sin(angles)], -1)
    return (cosine, sine)

def rotate(values, cosine, sine):
    half_dim = HD // 2
    turned = jnp.concatenate([-values[..., half_dim:], values[..., :half_dim]], -1)
    return values * cosine[:, None, :] + turned * sine[:, None, :]

def rms_norm(values, gain):
    scale = lax.rsqrt(lax.optimization_barrier(jnp.mean(values * values, -1, keepdims=True)) + epsilon)
    return values * scale * gain

def attend_one(queries, keys, values, length):
    group_size = HEADS // KV
    score_scale = 1.0 / math.sqrt(HD)
    grouped = queries.reshape(LEN, KV, group_size, HD)
    scores = jnp.einsum('qkgd,skd->kgqs', grouped, keys, precision=highest) * score_scale
    scores = low_back(scores)
    positions = jnp.arange(LEN)
    allowed = (positions[None, :] <= positions[:, None]) & (positions[None, :] < length)
    masked = jnp.where(allowed, scores, -1e+30)
    chances = low(jax.nn.softmax(masked, axis=-1))
    mixed = jnp.einsum('kgqs,skd->qkgd', chances, values, precision=highest)
    return low_back(low(mixed.reshape(LEN, HEADS * HD)))

def attend_pack(pack):
    return attend_one(*pack)

def forward(inputs, lens, first_gain, query_weight, key_weight, value_weight, out_weight, second_gain, gate_weight, up_weight, down_weight):
    count = lens.shape[0]
    cosine, sine = rope_tables()
    normed = low(rms_norm(inputs, low(first_gain)))
    query_lin = low_back(product(normed, low(query_weight)))
    key_lin = low_back(product(normed, low(key_weight)))
    values = low_back(low(product(normed, low(value_weight)))).reshape(count, LEN, KV, HD)
    queries = low(rotate(query_lin.reshape(count, LEN, HEADS, HD), cosine, sine))
    keys = low(rotate(key_lin.reshape(count, LEN, KV, HD), cosine, sine))
    mixed = lax.map(jax.checkpoint(attend_pack), (queries, keys, values, lens))
    mixed = mixed.reshape(count * LEN, HEADS * HD)
    attention = low_back(product(mixed, low(out_weight)))
    middle = inputs + attention
    normed_two = low(rms_norm(middle, low(second_gain)))
    gate = low_back(product(normed_two, low(gate_weight)))
    upper = low_back(product(normed_two, low(up_weight)))
    active = low(jax.nn.silu(gate) * upper)
    return middle + low_back(product(active, low(down_weight)))

def reference(tokens, lengths, first_gain, query_weight, key_weight, value_weight, out_weight, second_gain, gate_weight, up_weight, down_weight, cotangent):
    group_seqs = math.gcd(NSEQ, max(1, 4096 // LEN))
    groups = NSEQ // group_seqs
    rows = group_seqs * LEN
    params = (first_gain, query_weight, key_weight, value_weight, out_weight, second_gain, gate_weight, up_weight, down_weight)
    token_groups = tokens.astype(jnp.float32).reshape(groups, rows, D)
    cot_groups = cotangent.astype(jnp.float32).reshape(groups, rows, D)
    len_groups = lengths.reshape(groups, group_seqs)

    def step(carry, pack):
        token_block, len_block, cot_block = pack

        def local_forward(inputs, *weights):
            return forward(inputs, len_block, *weights)
        result, pullback = jax.vjp(local_forward, token_block, *params)
        positions = jnp.arange(rows) % LEN
        sequence_ids = jnp.arange(rows) // LEN
        valid = (positions < len_block[sequence_ids]).astype(jnp.float32)
        grads = pullback(cot_block * valid[:, None])
        carry = tuple((total + piece for total, piece in zip(carry, grads[1:])))
        return (carry, (result.astype(jnp.bfloat16), grads[0]))
    init = tuple((jnp.zeros_like(param) for param in params))
    sums, stacked = lax.scan(step, init, (token_groups, len_groups, cot_groups))
    outputs, input_grads = stacked
    return (outputs.reshape(TOKENS, D), input_grads.reshape(TOKENS, D), sums[0], sums[1], sums[2], sums[3], sums[4], sums[5], sums[6], sums[7], sums[8])
```

```python
import functools
import math

import jax
import jax.numpy as jnp
from jax import lax
from jax.experimental import pallas as pl
from jax.experimental.pallas import tpu as pltpu
from jax.sharding import PartitionSpec as P

HD = 80
LEN = 1024

epsilon = 1e-05
rope_base = 10000.0
masked_value = -1e30
score_scale = 1.0 / math.sqrt(HD)

BF = jnp.bfloat16
F32 = jnp.float32


def dot(spec, left, right):
    return jnp.einsum(spec, left, right, preferred_element_type=F32)


def rope_tables():
    half_dim = HD // 2
    freqs = rope_base ** (-(2.0 * jnp.arange(half_dim, dtype=F32)) / HD)
    angles = freqs[:, None] * jnp.arange(LEN, dtype=F32)[None, :]
    cosine, sine = jnp.cos(angles), jnp.sin(angles)
    return jnp.concatenate([cosine, cosine], 0), jnp.concatenate([sine, sine], 0)


def rms_scale(values):
    return lax.rsqrt(jnp.mean(values * values, -1, keepdims=True) + epsilon)


def line_chains(own):
    n = lax.axis_size("tensor")
    i = lax.axis_index("tensor")
    right, left = [own], [own]
    for s in range(1, n):
        right.append(lax.ppermute(right[-1], "tensor", [(j, j + 1) for j in range(s - 1, n - 1)]))
        left.append(lax.ppermute(left[-1], "tensor", [(j, j - 1) for j in range(1, n - s + 1)]))
    return [own] + [jnp.where(i >= s, right[s], left[n - s]) for s in range(1, n)]


def place(pieces):
    n = lax.axis_size("tensor")
    i = lax.axis_index("tensor")
    rows, width = pieces[0].shape
    out = jnp.zeros((n * rows, width), pieces[0].dtype)
    for s in range(n):
        out = lax.dynamic_update_slice(out, pieces[s], (((i - s) % n) * rows, 0))
    return out


def line_gather(own):
    return place(line_chains(own))


def line_scatter(part):
    n = lax.axis_size("tensor")
    i = lax.axis_index("tensor")
    rows = part.shape[0] // n

    def block(j):
        return lax.dynamic_slice(part, (jnp.clip(j, 0, n - 1) * rows, 0), (rows, part.shape[1]))

    sums = []
    for sign in (1, -1):
        held = None
        for t in range(1, n):
            term = block(i + sign * (n - t))
            if held is not None:
                term = (term.astype(F32) + held.astype(F32)).astype(BF)
            if sign > 0:
                pairs = [(j, j + 1) for j in range(t)]
            else:
                pairs = [(j, j - 1) for j in range(n - t, n)]
            held = lax.ppermute(term, "tensor", pairs)
        sums.append(held.astype(F32))
    return block(i).astype(F32) + sums[0] + sums[1]


def small_gather(own, axis):
    n = lax.axis_size(axis)
    i = lax.axis_index(axis)
    places = jnp.arange(n).reshape((n,) + (1,) * own.ndim)
    total = jnp.where(places == i, own[None], 0)
    for k in range(1, n):
        piece = lax.ppermute(own, axis, [(j, (j + k) % n) for j in range(n)])
        total = jnp.where(places == (i - k) % n, piece[None], total)
    return total


def turned(value):
    half = HD // 2
    return jnp.concatenate([-value[half:], value[:half]], 0)


def allowed_mask(key_count, query_start, query_count, length):
    keys = lax.broadcasted_iota(jnp.int32, (key_count, query_count), 0)
    places = lax.broadcasted_iota(jnp.int32, (key_count, query_count), 1) + query_start
    return (keys <= places) & (keys < length)


def forward_kernel(
    query_block, len_ref, q_ref, k_ref, v_ref, cos_ref, sin_ref, mixed_ref, roped_ref, log_ref,
    k_nat, heads, kv
):
    h = pl.program_id(0)
    group = heads // kv
    length = len_ref[0]
    cosine, sine = cos_ref[...], sin_ref[...]

    @pl.when(h % group == 0)
    def _():
        lin = k_ref[...]
        keys = (lin * cosine + turned(lin) * sine).astype(BF)
        at = pl.multiple_of((heads + h // group) * HD, 16)
        roped_ref[pl.ds(at, HD), :] = keys
        at = pl.multiple_of((heads + kv + h // group) * HD, 16)
        roped_ref[pl.ds(at, HD), :] = v_ref[...].astype(BF)
        k_nat[...] = keys.T

    lin = q_ref[...]
    queries = (lin * cosine + turned(lin) * sine).astype(BF)
    roped_ref[pl.ds(pl.multiple_of(h * HD, 16), HD), :] = queries
    values = v_ref[...].astype(BF)
    for start in range(0, LEN, query_block):
        count = start + query_block
        scores = jnp.dot(
            k_nat[:count, :], queries[:, start:count], preferred_element_type=F32
        ) * score_scale
        allowed = allowed_mask(count, start, query_block, length)
        masked = jnp.where(allowed, scores, masked_value)
        row_max = jnp.max(masked, 0, keepdims=True)
        powers = jnp.exp(masked - row_max)
        total = jnp.sum(powers, 0, keepdims=True)
        chances = (powers * (1.0 / total)).astype(BF)
        mixed = jnp.dot(values[:, :count], chances, preferred_element_type=F32)
        mixed_ref[:, start:count] = mixed.astype(BF)
        log_ref[pl.ds(h, 1), start:count] = row_max + jnp.log(total)


def attention_forward(lin, lengths, cosine, sine, heads, kv):
    group = heads // kv
    width = (heads + 2 * kv) * HD
    row = lambda f: pl.BlockSpec((HD, LEN), lambda h, n: (f(h), 0))
    whole = lambda shape: pl.BlockSpec(shape, lambda h, n: (0, 0))
    return pl.pallas_call(
        lambda *refs: forward_kernel(256, *refs, heads=heads, kv=kv),
        grid_spec=pltpu.PrefetchScalarGridSpec(
            num_scalar_prefetch=1,
            grid=(heads,),
            in_specs=[
                row(lambda h: h),
                row(lambda h: heads + h // group),
                row(lambda h: heads + kv + h // group),
                whole((HD, LEN)),
                whole((HD, LEN)),
            ],
            out_specs=[row(lambda h: h), whole((width, LEN)), whole((heads, LEN))],
            scratch_shapes=[pltpu.VMEM((LEN, HD), BF)],
        ),
        out_shape=[
            jax.ShapeDtypeStruct((heads * HD, LEN), BF),
            jax.ShapeDtypeStruct((width, LEN), BF),
            jax.ShapeDtypeStruct((heads, LEN), F32),
        ],
        cost_estimate=pl.CostEstimate(
            flops=heads * 4 * LEN * LEN * 128, bytes_accessed=8 << 20, transcendentals=heads * LEN * LEN
        ),
        name="attention_forward",
    )(lengths, lin, lin, lin, cosine, sine)


def backward_kernel(
    query_block, len_ref, q_ref, k_ref, v_ref, g_ref, log_ref, cos_ref, sin_ref, out_ref,
    k_nat, v_nat, k_acc, v_acc, heads, kv
):
    h = pl.program_id(0)
    group = heads // kv
    length = len_ref[0]
    cosine, sine = cos_ref[...], sin_ref[...]

    def unrope(grad):
        return (grad * cosine - turned(grad) * sine).astype(BF)

    @pl.when(h % group == 0)
    def _():
        k_nat[...] = k_ref[...].T
        v_nat[...] = v_ref[...].T
        k_acc[...] = jnp.zeros_like(k_acc)
        v_acc[...] = jnp.zeros_like(v_acc)

    pieces = []
    for start in range(0, LEN, query_block):
        count = start + query_block
        queries = q_ref[:, start:count]
        grads = g_ref[:, start:count]
        scores = jnp.dot(k_nat[:count, :], queries, preferred_element_type=F32) * score_scale
        allowed = allowed_mask(count, start, query_block, length)
        masked = jnp.where(allowed, scores, masked_value)
        chances = jnp.exp(masked - log_ref[pl.ds(h, 1), start:count])
        chance_grads = jnp.dot(v_nat[:count, :], grads, preferred_element_type=F32)
        delta = jnp.sum(chances * chance_grads, 0, keepdims=True)
        score_grads = (chances * (chance_grads - delta)).astype(BF)
        across = (((1,), (1,)), ((), ()))
        v_acc[:, :count] += lax.dot_general(
            grads, chances.astype(BF), across, preferred_element_type=F32
        )
        k_acc[:, :count] += lax.dot_general(
            queries, score_grads, across, preferred_element_type=F32
        )
        pieces.append(
            jnp.dot(k_ref[:, :count], score_grads, preferred_element_type=F32) * score_scale
        )
    out_ref[pl.ds(pl.multiple_of(h * HD, 16), HD), :] = unrope(jnp.concatenate(pieces, 1))

    @pl.when(h % group == group - 1)
    def _():
        at = pl.multiple_of((heads + h // group) * HD, 16)
        out_ref[pl.ds(at, HD), :] = unrope(k_acc[...] * score_scale)
        at = pl.multiple_of((heads + kv + h // group) * HD, 16)
        out_ref[pl.ds(at, HD), :] = v_acc[...].astype(BF)


def attention_backward(roped, head_grads, log_total, lengths, cosine, sine, heads, kv):
    group = heads // kv
    width = (heads + 2 * kv) * HD
    row = lambda f: pl.BlockSpec((HD, LEN), lambda h, n: (f(h), 0))
    whole = lambda shape: pl.BlockSpec(shape, lambda h, n: (0, 0))
    return pl.pallas_call(
        lambda *refs: backward_kernel(256, *refs, heads=heads, kv=kv),
        grid_spec=pltpu.PrefetchScalarGridSpec(
            num_scalar_prefetch=1,
            grid=(heads,),
            in_specs=[
                row(lambda h: h),
                row(lambda h: heads + h // group),
                row(lambda h: heads + kv + h // group),
                row(lambda h: h),
                whole((heads, LEN)),
                whole((HD, LEN)),
                whole((HD, LEN)),
            ],
            out_specs=whole((width, LEN)),
            scratch_shapes=[
                pltpu.VMEM((LEN, HD), BF),
                pltpu.VMEM((LEN, HD), BF),
                pltpu.VMEM((HD, LEN), F32),
                pltpu.VMEM((HD, LEN), F32),
            ],
        ),
        out_shape=jax.ShapeDtypeStruct((width, LEN), BF),
        cost_estimate=pl.CostEstimate(
            flops=heads * 10 * LEN * LEN * 128, bytes_accessed=8 << 20, transcendentals=heads * LEN * LEN
        ),
        name="attention_backward",
    )(lengths, roped, roped, roped, head_grads, log_total, cosine, sine)


def on_device(
    tokens,
    lengths,
    first_gain,
    query_weight,
    key_weight,
    value_weight,
    out_weight,
    second_gain,
    gate_weight,
    up_weight,
    down_weight,
    cotangent,
):
    rows_local = tokens.shape[0]
    assert lengths.shape[0] == 1 and rows_local * lax.axis_size("tensor") == LEN
    heads = query_weight.shape[1] // HD
    kv = key_weight.shape[1] // HD
    hidden = gate_weight.shape[1]
    place_t = lax.axis_index("tensor")

    token_pieces = line_chains(tokens)
    gains_own = jnp.stack([first_gain, second_gain]).astype(BF)
    gains = small_gather(gains_own, "dp")
    gains = jnp.swapaxes(gains, 0, 1).reshape(2, -1).astype(F32)
    first_float, second_float = gains[0:1], gains[1:2]

    attn_own = jnp.concatenate([query_weight, key_weight, value_weight], 1).astype(BF)
    out_own = out_weight.T.astype(BF)
    feed_own = jnp.concatenate([gate_weight, up_weight], 1).astype(BF)
    down_own = down_weight.T.astype(BF)
    gather = functools.partial(lax.all_gather, axis_name="dp", axis=0, tiled=True)
    attn_full = gather(attn_own)
    out_full = gather(out_own)
    feed_full = gather(feed_own)
    down_full = gather(down_own)

    def normed_of(piece):
        inputs = piece.astype(F32)
        return (inputs * rms_scale(inputs) * first_float).astype(BF)

    normed_all = place([normed_of(piece) for piece in token_pieces])
    inputs = tokens.astype(F32)
    first_scale = rms_scale(inputs)
    first_normed = inputs * first_scale
    cosine, sine = rope_tables()
    lin = dot("dq,rd->qr", attn_full, normed_all)
    mixed, roped, log_total = attention_forward(lin, lengths, cosine, sine, heads, kv)

    positions = place_t * rows_local + jnp.arange(rows_local)
    valid = (positions < lengths[0])[:, None]
    cot_own = jnp.where(valid, cotangent, jnp.zeros_like(cotangent))
    cot_later, lin = lax.optimization_barrier((cot_own, lin))
    feed_grads = line_gather(cot_later)
    out_grads = cot_own.astype(F32)

    attention = line_scatter(dot("qr,dq->rd", mixed, out_full).astype(BF))
    middle = inputs + attention
    second_scale = rms_scale(middle)
    second_normed = middle * second_scale
    hidden_in = line_gather((second_normed * second_float).astype(BF))
    gate_upper = dot("rd,df->rf", hidden_in, feed_full)
    active_grads = dot("rd,df->rf", feed_grads, down_full)
    gate, upper = gate_upper[:, :hidden], gate_upper[:, hidden:]
    sigma = jax.nn.sigmoid(gate)
    swish = gate * sigma
    active = (swish * upper).astype(BF)
    gate_grads = (active_grads * upper * sigma * (1.0 + gate * (1.0 - sigma))).astype(BF)
    upper_grads = (active_grads * swish).astype(BF)
    both_grads = jnp.concatenate([gate_grads, upper_grads], 1)
    second_back = line_scatter(dot("rf,df->rd", both_grads, feed_full).astype(BF))
    feed = line_scatter(dot("rf,df->rd", active, down_full).astype(BF))
    block_out = (middle + feed).astype(BF)
    second_ngrad = second_back * second_float
    middle_grads = out_grads + second_scale * (
        second_ngrad - second_normed * jnp.mean(second_ngrad * second_normed, -1, keepdims=True)
    )
    scatter = functools.partial(
        lax.psum_scatter, axis_name="dp", scatter_dimension=0, tiled=True
    )
    feed_share = scatter(dot("rd,rf->df", hidden_in, both_grads).astype(BF))
    down_share = scatter(dot("rd,rf->df", feed_grads, active).astype(BF))

    residual_all = line_gather(middle_grads.astype(BF))
    head_grads = dot("dq,rd->qr", out_full, residual_all).astype(BF)
    out_share = scatter(dot("rd,qr->dq", residual_all, mixed).astype(BF))
    attn_grads = attention_backward(
        roped, head_grads, log_total, lengths, cosine, sine, heads, kv
    )
    first_back = line_scatter(dot("qr,dq->rd", attn_grads, attn_full).astype(BF))
    attn_share = scatter(dot("rd,qr->dq", normed_all, attn_grads).astype(BF))
    first_ngrad = first_back * first_float
    tokens_grad = middle_grads + first_scale * (
        first_ngrad - first_normed * jnp.mean(first_ngrad * first_normed, -1, keepdims=True)
    )

    attn_share = attn_share.astype(F32)
    feed_share = feed_share.astype(F32)
    sums = jnp.stack(
        [
            jnp.sum(attn_share * attn_own.astype(F32), 1),
            jnp.sum(feed_share * feed_own.astype(F32), 1),
        ]
    ) / gains_own.astype(F32)
    totals = jnp.sum(small_gather(sums, "tensor"), 0)
    cut_q, cut_k = heads * HD, (heads + kv) * HD
    return (
        block_out,
        tokens_grad,
        totals[0],
        attn_share[:, :cut_q],
        attn_share[:, cut_q:cut_k],
        attn_share[:, cut_k:],
        out_share.astype(F32).T,
        totals[1],
        feed_share[:, :hidden],
        feed_share[:, hidden:],
        down_share.astype(F32).T,
    )


def solution(mesh):
    rows = P(("dp", "tensor"), None)
    split = P("dp", "tensor")
    turned_split = P("tensor", "dp")
    return jax.shard_map(
        on_device,
        mesh=mesh,
        in_specs=(
            rows, P("dp"), P("dp"), split, split, split, turned_split, P("dp"), split, split,
            turned_split, rows,
        ),
        out_specs=(
            rows, rows, P("dp"), split, split, split, turned_split, P("dp"), split, split,
            turned_split,
        ),
        check_vma=False,
    )
```

```python
import functools
import math

import jax
import jax.numpy as jnp
from jax import lax
from jax.experimental import pallas as pl
from jax.experimental.layout import Layout, with_layout_constraint
from jax.experimental.pallas import tpu as pltpu
from jax.sharding import PartitionSpec as P


HD = 80
LEN = 1024

epsilon = 1e-05
rope_base = 10000.0
masked_value = -1e30
CHUNKS = 2
score_scale = 1.0 / math.sqrt(HD)

BF = jnp.bfloat16
F32 = jnp.float32


def dot(spec, left, right):
    return jnp.einsum(spec, left, right, preferred_element_type=F32)


def rope_tables():
    half_dim = HD // 2
    freqs = rope_base ** (-(2.0 * jnp.arange(half_dim, dtype=F32)) / HD)
    angles = freqs[:, None] * jnp.arange(LEN, dtype=F32)[None, :]
    cosine, sine = jnp.cos(angles), jnp.sin(angles)
    return jnp.concatenate([cosine, cosine], 0), jnp.concatenate([sine, sine], 0)


def rms_scale(values):
    return lax.rsqrt(jnp.mean(values * values, -1, keepdims=True) + epsilon)


def line_chains(own):
    n = lax.axis_size("tensor")
    i = lax.axis_index("tensor")
    right, left = [own], [own]
    for s in range(1, n):
        right.append(lax.ppermute(right[-1], "tensor", [(j, j + 1) for j in range(s - 1, n - 1)]))
        left.append(
            lax.ppermute(left[-1], "tensor", [(j, j - 1) for j in range(1, n - s + 1)])
        )
    return [own] + [jnp.where(i >= s, right[s], left[n - s]) for s in range(1, n)]


def place(pieces):
    n = lax.axis_size("tensor")
    i = lax.axis_index("tensor")
    rows, width = pieces[0].shape
    out = jnp.zeros((n * rows, width), pieces[0].dtype)
    for s in range(n):
        out = lax.dynamic_update_slice(out, pieces[s], (((i - s) % n) * rows, 0))
    return out


def line_scatter(block, last_after=None):
    n = lax.axis_size("tensor")
    i = lax.axis_index("tensor")
    held = {1: None, -1: None}
    for t in range(1, n):
        for sign in (1, -1):
            term = block(jnp.clip(i + sign * (n - t), 0, n - 1))
            if held[sign] is not None:
                term = (term.astype(F32) + held[sign].astype(F32)).astype(BF)
            if t == n - 1 and last_after is not None:
                term, _ = lax.optimization_barrier((term, last_after))
            if sign > 0:
                pairs = [(j, j + 1) for j in range(t)]
            else:
                pairs = [(j, j - 1) for j in range(n - t, n)]
            held[sign] = lax.ppermute(term, "tensor", pairs)
    return block(i).astype(F32) + held[1].astype(F32) + held[-1].astype(F32)


def halving_scatter(part):
    dp = lax.axis_size("dp")
    i = lax.axis_index("dp")
    bits = dp.bit_length() - 1
    assert dp == 1 << bits
    rows, width = part.shape[0] // dp, part.shape[1]

    def step(value, order, bit):
        axis = order.index(bit)
        mine = (i >> bit) & 1
        send = lax.dynamic_index_in_dim(value, 1 - mine, axis, keepdims=False)
        keep = lax.dynamic_index_in_dim(value, mine, axis, keepdims=False)
        got = lax.ppermute(send, "dp", [(j, j ^ (1 << bit)) for j in range(dp)])
        total = (keep.astype(F32) + got.astype(F32)).astype(BF)
        return total, [o for o in order if o != bit]

    order = list(range(bits - 1, -1, -1))
    part = with_layout_constraint(part, Layout(major_to_minor=(0, 1)))
    value, order = step(part.reshape((2,) * bits + (rows, width)), order, 0)
    outs = []
    for k in range(2):
        piece, left = value[..., k * (rows // 2) : (k + 1) * (rows // 2), :], order
        for bit in range(1, bits) if k == 0 else range(bits - 1, 0, -1):
            piece, left = step(piece, left, bit)
        outs.append(piece)
    return jnp.concatenate(outs, 0)


def small_gather(own, axis):
    n = lax.axis_size(axis)
    i = lax.axis_index(axis)
    places = jnp.arange(n).reshape((n,) + (1,) * own.ndim)
    total = jnp.where(places == i, own[None], 0)
    for k in range(1, n):
        piece = lax.ppermute(own, axis, [(j, (j + k) % n) for j in range(n)])
        total = jnp.where(places == (i - k) % n, piece[None], total)
    return total


def turned(value):
    half = HD // 2
    return jnp.concatenate([-value[half:], value[:half]], 0)


def allowed_mask(key_count, query_start, query_count, length):
    keys = lax.broadcasted_iota(jnp.int32, (key_count, query_count), 0)
    places = lax.broadcasted_iota(jnp.int32, (key_count, query_count), 1) + query_start
    return (keys <= places) & (keys < length)


def forward_kernel(
    query_block, len_ref, q_ref, k_ref, v_ref, cos_ref, sin_ref, mixed_ref, roped_ref, log_ref,
    k_nat, heads, kv
):
    h = pl.program_id(0)
    group = heads // kv
    length = len_ref[0]
    cosine, sine = cos_ref[...], sin_ref[...]

    @pl.when(h % group == 0)
    def _():
        lin = k_ref[...]
        keys = (lin * cosine + turned(lin) * sine).astype(BF)
        at = pl.multiple_of((heads + h // group) * HD, 16)
        roped_ref[pl.ds(at, HD), :] = keys
        at = pl.multiple_of((heads + kv + h // group) * HD, 16)
        roped_ref[pl.ds(at, HD), :] = v_ref[...].astype(BF)
        k_nat[...] = keys.T

    lin = q_ref[...]
    queries = (lin * cosine + turned(lin) * sine).astype(BF)
    roped_ref[pl.ds(pl.multiple_of(h * HD, 16), HD), :] = queries
    values = v_ref[...].astype(BF)
    for start in range(0, LEN, query_block):
        count = start + query_block
        scores = jnp.dot(
            k_nat[:count, :], queries[:, start:count], preferred_element_type=F32
        ) * score_scale
        allowed = allowed_mask(count, start, query_block, length)
        masked = jnp.where(allowed, scores, masked_value)
        row_max = jnp.max(masked, 0, keepdims=True)
        powers = jnp.exp(masked - row_max)
        total = jnp.sum(powers, 0, keepdims=True)
        chances = (powers * (1.0 / total)).astype(BF)
        mixed = jnp.dot(values[:, :count], chances, preferred_element_type=F32)
        mixed_ref[:, start:count] = mixed.astype(BF)
        log_ref[pl.ds(h, 1), start:count] = row_max + jnp.log(total)


def attention_forward(lin, lengths, cosine, sine, heads, kv):
    group = heads // kv
    width = (heads + 2 * kv) * HD
    row = lambda f: pl.BlockSpec((HD, LEN), lambda h, n: (f(h), 0))
    whole = lambda shape: pl.BlockSpec(shape, lambda h, n: (0, 0))
    return pl.pallas_call(
        lambda *refs: forward_kernel(256, *refs, heads=heads, kv=kv),
        grid_spec=pltpu.PrefetchScalarGridSpec(
            num_scalar_prefetch=1,
            grid=(heads,),
            in_specs=[
                row(lambda h: h),
                row(lambda h: heads + h // group),
                row(lambda h: heads + kv + h // group),
                whole((HD, LEN)),
                whole((HD, LEN)),
            ],
            out_specs=[row(lambda h: h), whole((width, LEN)), whole((heads, LEN))],
            scratch_shapes=[pltpu.VMEM((LEN, HD), BF)],
        ),
        out_shape=[
            jax.ShapeDtypeStruct((heads * HD, LEN), BF),
            jax.ShapeDtypeStruct((width, LEN), BF),
            jax.ShapeDtypeStruct((heads, LEN), F32),
        ],
        cost_estimate=pl.CostEstimate(
            flops=heads * 4 * LEN * LEN * 128, bytes_accessed=8 << 20, transcendentals=heads * LEN * LEN
        ),
        name="attention_forward",
    )(lengths, lin, lin, lin, cosine, sine)


def backward_kernel(
    query_block, len_ref, q_ref, k_ref, v_ref, g_ref, log_ref, cos_ref, sin_ref, out_ref,
    k_nat, v_nat, k_acc, v_acc, heads, kv
):
    h = pl.program_id(0)
    group = heads // kv
    length = len_ref[0]
    cosine, sine = cos_ref[...], sin_ref[...]

    def unrope(grad):
        return (grad * cosine - turned(grad) * sine).astype(BF)

    @pl.when(h % group == 0)
    def _():
        k_nat[...] = k_ref[...].T
        v_nat[...] = v_ref[...].T
        k_acc[...] = jnp.zeros_like(k_acc)
        v_acc[...] = jnp.zeros_like(v_acc)

    pieces = []
    for start in range(0, LEN, query_block):
        count = start + query_block
        queries = q_ref[:, start:count]
        grads = g_ref[:, start:count]
        scores = jnp.dot(k_nat[:count, :], queries, preferred_element_type=F32) * score_scale
        allowed = allowed_mask(count, start, query_block, length)
        masked = jnp.where(allowed, scores, masked_value)
        chances = jnp.exp(masked - log_ref[pl.ds(h, 1), start:count])
        chance_grads = jnp.dot(v_nat[:count, :], grads, preferred_element_type=F32)
        delta = jnp.sum(chances * chance_grads, 0, keepdims=True)
        score_grads = (chances * (chance_grads - delta)).astype(BF)
        across = (((1,), (1,)), ((), ()))
        v_acc[:, :count] += lax.dot_general(
            grads, chances.astype(BF), across, preferred_element_type=F32
        )
        k_acc[:, :count] += lax.dot_general(
            queries, score_grads, across, preferred_element_type=F32
        )
        pieces.append(
            jnp.dot(k_ref[:, :count], score_grads, preferred_element_type=F32) * score_scale
        )
    out_ref[pl.ds(pl.multiple_of(h * HD, 16), HD), :] = unrope(jnp.concatenate(pieces, 1))

    @pl.when(h % group == group - 1)
    def _():
        at = pl.multiple_of((heads + h // group) * HD, 16)
        out_ref[pl.ds(at, HD), :] = unrope(k_acc[...] * score_scale)
        at = pl.multiple_of((heads + kv + h // group) * HD, 16)
        out_ref[pl.ds(at, HD), :] = v_acc[...].astype(BF)


def attention_backward(roped, head_grads, log_total, lengths, cosine, sine, heads, kv):
    group = heads // kv
    width = (heads + 2 * kv) * HD
    row = lambda f: pl.BlockSpec((HD, LEN), lambda h, n: (f(h), 0))
    whole = lambda shape: pl.BlockSpec(shape, lambda h, n: (0, 0))
    return pl.pallas_call(
        lambda *refs: backward_kernel(256, *refs, heads=heads, kv=kv),
        grid_spec=pltpu.PrefetchScalarGridSpec(
            num_scalar_prefetch=1,
            grid=(heads,),
            in_specs=[
                row(lambda h: h),
                row(lambda h: heads + h // group),
                row(lambda h: heads + kv + h // group),
                row(lambda h: h),
                whole((heads, LEN)),
                whole((HD, LEN)),
                whole((HD, LEN)),
            ],
            out_specs=whole((width, LEN)),
            scratch_shapes=[
                pltpu.VMEM((LEN, HD), BF),
                pltpu.VMEM((LEN, HD), BF),
                pltpu.VMEM((HD, LEN), F32),
                pltpu.VMEM((HD, LEN), F32),
            ],
        ),
        out_shape=jax.ShapeDtypeStruct((width, LEN), BF),
        cost_estimate=pl.CostEstimate(
            flops=heads * 10 * LEN * LEN * 128, bytes_accessed=8 << 20, transcendentals=heads * LEN * LEN
        ),
        name="attention_backward",
    )(lengths, roped, roped, roped, head_grads, log_total, cosine, sine)


def layer(
    tokens,
    lengths,
    first_gain,
    query_weight,
    key_weight,
    value_weight,
    out_weight,
    second_gain,
    gate_weight,
    up_weight,
    down_weight,
    cotangent,
):
    rows_local = tokens.shape[0]
    assert lengths.shape[0] == 1 and rows_local * lax.axis_size("tensor") == LEN
    heads = query_weight.shape[1] // HD
    kv = key_weight.shape[1] // HD
    hidden = gate_weight.shape[1]
    place_t = lax.axis_index("tensor")

    chunk = rows_local // CHUNKS
    chunks = range(CHUNKS)

    def cut(value, c):
        return value[c * chunk : (c + 1) * chunk]

    token_pieces = line_chains(tokens)
    gains_own = jnp.stack([first_gain, second_gain]).astype(BF)
    gains = small_gather(gains_own, "dp")
    gains, query_weight, key_weight, value_weight, out_weight, gate_weight, up_weight, down_weight = (
        lax.optimization_barrier(
            (
                gains, query_weight, key_weight, value_weight, out_weight, gate_weight, up_weight,
                down_weight,
            )
        )
    )
    gains = jnp.swapaxes(gains, 0, 1).reshape(2, -1).astype(F32)
    first_float, second_float = gains[0:1], gains[1:2]

    attn_own = jnp.concatenate([query_weight, key_weight, value_weight], 1).astype(BF)
    out_own = out_weight.T.astype(BF)
    feed_own = jnp.concatenate([gate_weight, up_weight], 1).astype(BF)
    down_own = down_weight.T.astype(BF)
    gather = functools.partial(lax.all_gather, axis_name="dp", axis=0, tiled=True)
    attn_full = gather(attn_own)
    out_full = gather(out_own)
    feed_full = gather(feed_own)
    down_full = gather(down_own)

    def normed_of(piece):
        inputs = piece.astype(F32)
        return (inputs * rms_scale(inputs) * first_float).astype(BF)

    normed_all = place([normed_of(piece) for piece in token_pieces])
    group_gather = functools.partial(lax.all_gather, axis_name="tensor", axis=0, tiled=True)
    group_scatter = functools.partial(
        lax.psum_scatter, axis_name="tensor", scatter_dimension=0, tiled=True
    )
    inputs = tokens.astype(F32)
    first_scale = rms_scale(inputs)
    first_normed = inputs * first_scale
    cosine, sine = rope_tables()
    lin = dot("dq,rd->qr", attn_full, normed_all)
    mixed, roped, log_total = attention_forward(lin, lengths, cosine, sine, heads, kv)

    positions = place_t * rows_local + jnp.arange(rows_local)
    valid = (positions < lengths[0])[:, None]
    cot_own = jnp.where(valid, cotangent, jnp.zeros_like(cotangent))
    out_grads = cot_own.astype(F32)
    cot_later, _ = lax.optimization_barrier((cot_own, token_pieces[-1]))
    cot_pieces = line_chains(cot_later)
    feed_grads = [place([cut(piece, c) for piece in cot_pieces]) for c in chunks]

    mixed_out = dot("qr,dq->rd", mixed, out_full).astype(BF)
    width = mixed_out.shape[1]

    def mixed_block(j):
        return lax.dynamic_slice(mixed_out, (j * rows_local, 0), (rows_local, width))

    middle = inputs + line_scatter(mixed_block)
    second_scale = rms_scale(middle)
    second_normed = middle * second_scale
    hidden_own = (second_normed * second_float).astype(BF)
    hidden_own, feed_full, down_full = lax.optimization_barrier((hidden_own, feed_full, down_full))
    hidden_in = [group_gather(cut(hidden_own, c)) for c in chunks]
    active, both_grads, second_back = [], [], []
    for c in chunks:
        gate_upper = dot("rd,df->rf", hidden_in[c], feed_full)
        active_grads = dot("rd,df->rf", feed_grads[c], down_full)
        gate, upper = gate_upper[:, :hidden], gate_upper[:, hidden:]
        sigma = jax.nn.sigmoid(gate)
        swish = gate * sigma
        active.append((swish * upper).astype(BF))
        gate_grads = (active_grads * upper * sigma * (1.0 + gate * (1.0 - sigma))).astype(BF)
        upper_grads = (active_grads * swish).astype(BF)
        both_grads.append(jnp.concatenate([gate_grads, upper_grads], 1))
        second_back.append(group_scatter(dot("rf,df->rd", both_grads[c], feed_full).astype(BF)))
    second_back = jnp.concatenate(second_back, 0)
    hidden_all = jnp.concatenate(hidden_in, 0)
    both_all = jnp.concatenate(both_grads, 0)
    active_all = jnp.concatenate(active, 0)
    feed_grads_all = jnp.concatenate(feed_grads, 0)
    feed_part = dot("rf,df->rd", active_all, down_full).astype(BF)
    feed_part, second_back = lax.optimization_barrier((feed_part, second_back))
    second_back = second_back.astype(F32)
    second_ngrad = second_back * second_float
    middle_grads = out_grads + second_scale * (
        second_ngrad - second_normed * jnp.mean(second_ngrad * second_normed, -1, keepdims=True)
    )
    residual_all = group_gather(middle_grads.astype(BF))
    feed_share = halving_scatter(dot("rd,rf->df", hidden_all, both_all).astype(BF))
    down_share = halving_scatter(dot("rd,rf->df", feed_grads_all, active_all).astype(BF))

    def feed_block(j):
        return jnp.concatenate(
            [
                lax.dynamic_slice(feed_part, (c * (LEN // CHUNKS) + j * chunk, 0), (chunk, width))
                for c in chunks
            ],
            0,
        )

    feed = line_scatter(feed_block, residual_all)
    block_out = (middle + feed).astype(BF)

    head_grads = dot("dq,rd->qr", out_full, residual_all).astype(BF)
    out_share = halving_scatter(dot("rd,qr->dq", residual_all, mixed).astype(BF))
    attn_grads = attention_backward(roped, head_grads, log_total, lengths, cosine, sine, heads, kv)
    first_back = group_scatter(dot("qr,dq->rd", attn_grads, attn_full).astype(BF)).astype(F32)
    attn_share = halving_scatter(dot("rd,qr->dq", normed_all, attn_grads).astype(BF))
    first_ngrad = first_back * first_float
    tokens_grad = middle_grads + first_scale * (
        first_ngrad - first_normed * jnp.mean(first_ngrad * first_normed, -1, keepdims=True)
    )

    attn_share = attn_share.astype(F32)
    feed_share = feed_share.astype(F32)
    sums = jnp.stack(
        [
            jnp.sum(attn_share * attn_own.astype(F32), 1),
            jnp.sum(feed_share * feed_own.astype(F32), 1),
        ]
    ) / gains_own.astype(F32)
    totals = jnp.sum(small_gather(sums, "tensor"), 0)
    cut_q, cut_k = heads * HD, (heads + kv) * HD
    return (
        block_out,
        tokens_grad,
        totals[0],
        attn_share[:, :cut_q],
        attn_share[:, cut_q:cut_k],
        attn_share[:, cut_k:],
        out_share.astype(F32).T,
        totals[1],
        feed_share[:, :hidden],
        feed_share[:, hidden:],
        down_share.astype(F32).T,
    )


def solution(mesh):
    rows = P(("dp", "tensor"), None)
    split = P("dp", "tensor")
    turned_split = P("tensor", "dp")
    return jax.shard_map(
        layer,
        mesh=mesh,
        in_specs=(
            rows, P("dp"), P("dp"), split, split, split, turned_split, P("dp"), split, split,
            turned_split, rows,
        ),
        out_specs=(
            rows, rows, P("dp"), split, split, split, turned_split, P("dp"), split, split,
            turned_split,
        ),
        check_vma=False,
    )
```
